32 devices in a mesh: seq: 16 (over z, x, core), ex: 2 (over y).
Axes of the slice: x: 2, y: 2, z: 4, core: 2. Of those that a mesh axis runs over, the one named last changes fastest.
Arguments:
- acts: bfloat16 [4, 2048, 4096], P('ex', 'seq'), may hold values from -6 to 6
- out_grads: bfloat16 [4, 2048, 5120], P('ex', 'seq'), may hold values from -6 to 6
- lengths: int32 [4], P('ex'), may hold values from 512 to 2048, as said below
- in_tiles: bfloat16 [32, 128, 128], replicated, may hold values from -0.09375 to 0.09375
- in_blocks: int32 [32], replicated, may hold values from 0 to 31, each once
- in_signs: int32 [32, 128], replicated, may hold values 0 or 1
- out_tiles: bfloat16 [40, 128, 64], replicated, may hold values from -0.09375 to 0.09375
- out_blocks: int32 [40], replicated, may hold values from 0 to 39, as said below
- out_signs: int32 [40, 128], replicated, may hold values 0 or 1
- query_grads: bfloat16 [2048, 8192], P('seq', 'ex'), may hold values from -6 to 6
Outputs:
- scores: float32 [4, 2048], P('ex', 'seq')
The draws below stay inside these ranges and needn't reach their ends.
Inputs may be any that keep to these rules, and one draw needn't show every extreme that they name: `lengths`: every training sequence has at least 512 live positions and some sequence has all 2048. `in_blocks`: a permutation of the 32 input feature blocks. `out_blocks`: the first 32 entries are a permutation of 0 to 31, the last 8 a permutation of 32 to 39.
All inputs are finite; a program needn't handle non-finite values.
Results may differ from the reference program's by a relative error of at most 0.005.
Values may be sent and summed in bfloat16 or wider, within the bound.
A program may use at most 64 MiB of HBM per device.

```python
import jax
import jax.numpy as jnp
from jax import lax

D = 4096
KV = 1024
S = 2048
KI = 64
KO = 64
EXAMPLES = 4
QUERIES = 2048
PROJ = 8192


def draw_lengths(key, part):
    base = jax.random.randint(jax.random.fold_in(key, 11), (EXAMPLES,), S // 4, S + 1)
    longest = jax.random.randint(jax.random.fold_in(key, 12), (), 0, EXAMPLES)
    return jnp.where(jnp.arange(EXAMPLES) == longest, S, base).astype(jnp.int32)


def draw_out_blocks(key, part):
    upper = jax.random.permutation(jax.random.fold_in(key, 21), D // 128)
    lower = D // 128 + jax.random.permutation(jax.random.fold_in(key, 22), KV // 128)
    return jnp.concatenate([upper, lower]).astype(jnp.int32)


def plant(array, stream_key, smallest, largest):
    longest = array.shape.index(max(array.shape))
    spots = []
    for shift in (0, 1):
        where = [jax.random.randint(jax.random.fold_in(stream_key, axis), (), 0, length) for axis, length in enumerate(array.shape)]
        where[longest] = (where[longest] + shift) % array.shape[longest]
        spots.append(tuple(where))
    return array.at[spots[0]].set(smallest).at[spots[1]].set(largest)


def block_levels(own_key, extent, cuts, smallest, largest):
    def one(axis_at, parts):
        heights = jax.random.uniform(jax.random.fold_in(jax.random.fold_in(own_key, 6), axis_at), (parts,), jnp.float32, smallest / len(cuts), largest / len(cuts))
        return jnp.repeat(jnp.exp(heights), extent[axis_at] // parts).reshape((-1,) + (1,) * (len(extent) - axis_at - 1))

    factor_of = one(*cuts[0])
    for cut in cuts[1:]:
        factor_of = factor_of * one(*cut)
    return factor_of


def gaussian(stream_key, dims, spread, most, pieces=(), kind=jnp.bfloat16):
    drawn = jax.random.normal(stream_key, dims, jnp.float32) * spread
    if len(pieces) > 0:
        drawn = block_levels(stream_key, dims, pieces, -0.22, 0.18) * drawn
    return jnp.clip(drawn, min=-most, max=most).astype(kind)


def setup_inputs(seed: int = 0) -> dict:
    key_list = jax.random.split(jax.random.key(seed), 11)
    return {
        "acts": gaussian(key_list[0], (EXAMPLES, S, D), 1.0, 6.0, ((0, 2), (1, 16))),
        "out_grads": gaussian(key_list[1], (EXAMPLES, S, D + KV), 1.0, 6.0, ((0, 2), (1, 16))),
        "lengths": draw_lengths(jax.random.fold_in(key_list[10], 71), 0),
        "in_tiles": gaussian(key_list[3], (D // 128, 128, 2 * KI), D ** -0.5, 0.09375),
        "in_blocks": jax.random.permutation(key_list[4], D // 128).astype(jnp.int32),
        "in_signs": plant((jax.random.randint(key_list[5], (D // 128, 128), 0, 2) < 1).astype(jnp.int32), jax.random.fold_in(key_list[5], 1), 0, 1),
        "out_tiles": gaussian(key_list[6], ((D + KV) // 128, 128, KO), D ** -0.5, 0.09375),
        "out_blocks": draw_out_blocks(jax.random.fold_in(key_list[10], 71), 0),
        "out_signs": plant((jax.random.randint(key_list[8], ((D + KV) // 128, 128), 0, 2) < 1).astype(jnp.int32), jax.random.fold_in(key_list[8], 1), 0, 1),
        "query_grads": gaussian(key_list[9], (QUERIES, PROJ), 1.0, 6.0, ((0, 16), (1, 2))),
    }


def place(sketch_tiles, block_ids, sign_bits):
    signed = sketch_tiles.astype(jnp.float32) * (2 * sign_bits - 1).astype(jnp.float32)[:, :, None]
    placed = jnp.zeros_like(signed).at[block_ids].set(signed)
    return placed.reshape(-1, sketch_tiles.shape[2]).astype(jnp.bfloat16)


def widen(placed, split_at):
    out_cols = placed.shape[1]
    upper = jnp.concatenate([placed[:split_at], jnp.zeros((split_at, out_cols), jnp.bfloat16)], 1)
    lower = jnp.concatenate([jnp.zeros((placed.shape[0] - split_at, out_cols), jnp.bfloat16), placed[split_at:]], 1)
    return jnp.concatenate([upper, lower], 0)


def reference(acts, out_grads, lengths, in_tiles, in_blocks, in_signs, out_tiles, out_blocks, out_signs, query_grads):
    r_in = place(in_tiles, in_blocks, in_signs)
    r_out = widen(place(out_tiles, out_blocks, out_signs), D)
    positions = jnp.arange(S, dtype=jnp.int32)

    def per_example(example):
        act_rows, grad_rows, seq_length = example
        live_rows = (positions < seq_length).astype(jnp.float32)
        in_sketched = (jnp.dot(act_rows, r_in, preferred_element_type=jnp.float32) * live_rows[:, None]).astype(jnp.bfloat16)
        out_sketched = jnp.dot(grad_rows, r_out, preferred_element_type=jnp.float32).astype(jnp.bfloat16)
        crossed = jnp.dot(in_sketched.T, out_sketched, preferred_element_type=jnp.float32)
        joined = jnp.stack([crossed[:KI, :KO], crossed[KI:, KO:]], 0).reshape(-1)
        return joined / seq_length.astype(jnp.float32)

    train_proj = lax.map(per_example, (acts, out_grads, lengths)).astype(jnp.bfloat16)
    return jnp.dot(train_proj, query_grads.T, preferred_element_type=jnp.float32)
```

```python
import functools

import jax
import jax.numpy as jnp
from jax import lax
from jax.experimental import pallas as pl
from jax.experimental.pallas import tpu as pltpu
from jax.sharding import PartitionSpec as P

MESH = pl.DeviceIdType.MESH
SUBLANES = 16


def signed_columns(rows_ref, blocks_ref, signs_ref, first, count):
    _, examples, positions, width = rows_ref.shape
    signs = (2 * signs_ref[...] - 1).astype(jnp.float32).astype(jnp.bfloat16)
    columns = []
    for b in range(first, first + count):
        block = rows_ref[blocks_ref[b]].reshape(examples * positions, width)
        columns.append(block * signs[b : b + 1, :])
    return jnp.concatenate(columns, axis=1)


def body(
    seq_count,
    ex_count,
    inner,
    lengths_ref,
    in_blocks_ref,
    out_blocks_ref,
    acts_hbm,
    grads_hbm,
    in_tiles_hbm,
    in_signs_hbm,
    out_tiles_hbm,
    out_signs_hbm,
    query_hbm,
    out_ref,
    acts,
    grads,
    in_tiles,
    in_signs,
    out_tiles,
    out_signs,
    query,
    pieces,
    a_recv,
    b_send,
    b_recv,
    ordered,
    c_send,
    c_recv,
    d_send,
    d_recv,
    load_sem,
    a_ssem,
    a_rsem,
    b_ssem,
    b_rsem,
    c_ssem,
    c_rsem,
    d_ssem,
    d_rsem,
):
    outer = seq_count // inner
    s = lax.axis_index("seq")
    x = lax.axis_index("ex")
    o = s // inner
    i = lax.rem(s, inner)

    loads = {}
    for n, (name, src, dst) in enumerate(
        (
            ("in_signs", in_signs_hbm, in_signs),
            ("out_signs", out_signs_hbm, out_signs),
            ("in_tiles", in_tiles_hbm, in_tiles),
            ("acts", acts_hbm, acts),
            ("out_tiles", out_tiles_hbm, out_tiles),
            ("grads", grads_hbm, grads),
            ("query", query_hbm, query),
        )
    ):
        if src.shape == dst.shape:
            loads[name] = pltpu.make_async_copy(src, dst, load_sem.at[n])
            loads[name].start()
            continue
        width = dst.shape[3]
        for b in range(dst.shape[0]):
            pltpu.make_async_copy(
                src.at[:, :, b * width : (b + 1) * width], dst.at[b], load_sem.at[n]
            ).start()
        loads[name] = pltpu.make_async_copy(dst, dst, load_sem.at[n])

    def at(outer_step, inner_step, ex_step):
        to_o = lax.rem(o + outer_step, outer)
        to_i = lax.rem(i + inner_step, inner)
        to_x = lax.rem(x + ex_step, ex_count)
        return to_o * inner + to_i, to_x

    near = [(di, dx) for dx in range(ex_count) for di in range(inner) if di or dx]
    barrier = pltpu.get_barrier_semaphore()
    peers = [(0, di, dx) for di, dx in near] + [(do, 0, 0) for do in range(1, outer)]
    for steps in peers:
        to_s, to_x = at(*steps)
        pl.semaphore_signal(barrier, 1, device_id=(to_s, to_x), device_id_type=MESH)

    _, examples, positions, _ = acts.shape
    in_count = in_tiles.shape[0]
    out_count = out_tiles.shape[0]
    cols = out_tiles.shape[1]
    f32 = jnp.float32

    loads["in_signs"].wait()
    loads["in_tiles"].wait()
    loads["acts"].wait()
    left = signed_columns(acts, in_blocks_ref, in_signs, 0, in_count)
    tiles = in_tiles[...].reshape(-1, in_tiles.shape[2])
    in_sketched = jnp.dot(left, tiles, preferred_element_type=f32)
    place = s * positions + lax.broadcasted_iota(jnp.int32, (positions, 1), 0)
    in_parts = [
        jnp.where(
            place < lengths_ref[e], in_sketched[e * positions : (e + 1) * positions], 0.0
        ).astype(jnp.bfloat16)
        for e in range(examples)
    ]

    loads["out_signs"].wait()
    loads["out_tiles"].wait()
    loads["grads"].wait()
    upper = signed_columns(grads, out_blocks_ref, out_signs, 0, in_count)
    lower = signed_columns(grads, out_blocks_ref, out_signs, in_count, out_count - in_count)
    halves = [
        lax.dot_general(
            left,
            jnp.concatenate([out_tiles[b] for b in range(first, last)], axis=1),
            (((1,), (1,)), ((), ())),
            preferred_element_type=f32,
        ).astype(jnp.bfloat16)
        for left, first, last in ((upper, 0, in_count), (lower, in_count, out_count))
    ]

    half_rows = in_parts[0].shape[1] // 2
    piece_rows = pieces.shape[1]
    crossed = [[], []]
    for e in range(examples):
        out_part = jnp.concatenate(
            [half[e * positions : (e + 1) * positions] for half in halves], axis=1
        )
        full = lax.dot_general(
            in_parts[e], out_part, (((0,), (0,)), ((), ())), preferred_element_type=f32
        )
        full = full / lengths_ref[e].astype(f32)
        crossed[0].append(full[:half_rows, :cols])
        crossed[1].append(full[half_rows:, cols:])
    joined = jnp.concatenate([jnp.concatenate(part, axis=1) for part in crossed], axis=0)
    for p in range(pieces.shape[0]):
        pieces[p] = joined[p * piece_rows : (p + 1) * piece_rows]

    pl.semaphore_wait(barrier, len(peers))

    sends = []

    def push(src, dst, ssem, rsem, steps):
        to_s, to_x = at(*steps)
        copy = pltpu.make_async_remote_copy(
            src, dst, ssem, rsem, device_id=(to_s, to_x), device_id_type=MESH
        )
        copy.start()
        sends.append(copy)
        return copy

    got = {}
    for di, dx in near:
        to_i = lax.rem(i + di, inner)
        to_x = lax.rem(x + dx, ex_count)
        slot = dx * inner + di
        got[slot] = push(
            pieces.at[to_x * inner + to_i],
            a_recv.at[slot],
            a_ssem.at[slot],
            a_rsem.at[slot],
            (0, di, dx),
        )
    own = pieces[x * inner + i]
    for dx in range(ex_count):
        total = own if dx == 0 else None
        for di in range(inner):
            slot = dx * inner + di
            if slot == 0:
                continue
            got[slot].wait_recv()
            total = a_recv[slot] if total is None else total + a_recv[slot]
        b_send[dx] = total

    arrivals = [
        push(b_send, b_recv.at[do], b_ssem.at[do], b_rsem.at[do], (do, 0, 0))
        for do in range(1, outer)
    ]
    summed = b_send[...]
    for do, copy in enumerate(arrivals, 1):
        copy.wait_recv()
        summed = summed + b_recv[do]
    b_recv[0] = summed

    all_examples = ex_count * examples
    pairs = piece_rows // 2
    for dx in range(ex_count):
        even = b_recv[0, dx, pl.ds(0, pairs, stride=2), :]
        odd = b_recv[0, dx, pl.ds(1, pairs, stride=2), :]
        for e in range(examples):
            lanes = slice(e * cols, (e + 1) * cols)
            ordered[pl.ds(dx * examples + e, pairs, stride=all_examples), :] = jnp.concatenate(
                [even[:, lanes], odd[:, lanes]], axis=1
            )
    c_send[...] = ordered[...].astype(jnp.bfloat16)
    arrivals = [
        push(c_send, c_recv.at[di], c_ssem.at[di], c_rsem.at[di], (0, di, 0))
        for di in range(1, inner)
    ]

    loads["query"].wait()
    width = 2 * cols
    group = max(SUBLANES, all_examples)
    per_group = group // all_examples
    groups = c_send.shape[0] // group
    sums = [None] * per_group
    for di in range(inner):
        if di:
            arrivals[di - 1].wait_recv()
        from_i = lax.rem(i - di + inner, inner)
        chunk = c_recv[di] if di else c_send[...]
        left = jnp.concatenate(
            [chunk[u * group : (u + 1) * group] for u in range(groups)], axis=1
        )
        for j in range(per_group):
            right = jnp.concatenate(
                [
                    query[
                        :,
                        pl.ds(
                            pl.multiple_of((from_i * pairs + u * per_group + j) * width, width),
                            width,
                        ),
                    ]
                    for u in range(groups)
                ],
                axis=1,
            )
            term = lax.dot_general(
                left, right, (((1,), (1,)), ((), ())), preferred_element_type=f32
            )
            sums[j] = term if sums[j] is None else sums[j] + term
    scores = sums[0][:all_examples]
    for j in range(1, per_group):
        scores = scores + sums[j][j * all_examples : (j + 1) * all_examples]

    for dx in range(1, ex_count):
        d_send[dx] = scores[dx * examples : (dx + 1) * examples]
    arrivals = [
        push(
            d_send.at[dx], d_recv.at[dx], d_ssem.at[dx], d_rsem.at[dx], (0, 0, ex_count - dx)
        )
        for dx in range(1, ex_count)
    ]
    result = scores[:examples]
    for dx, copy in enumerate(arrivals, 1):
        copy.wait_recv()
        result = result + d_recv[dx]
    out_ref[...] = result
    for copy in sends:
        copy.wait_send()


def per_device(
    seq_count,
    ex_count,
    acts,
    out_grads,
    lengths,
    in_tiles,
    in_blocks,
    in_signs,
    out_tiles,
    out_blocks,
    out_signs,
    query_grads,
):
    examples = acts.shape[0]
    queries = query_grads.shape[0]
    in_cols = in_tiles.shape[2]
    cols = out_tiles.shape[2]
    inner = 4 if seq_count % 4 == 0 else 1
    outer = seq_count // inner
    piece_rows = in_cols // (ex_count * inner)
    lanes = examples * cols
    gathered = piece_rows // 2 * ex_count * examples
    smem = pl.BlockSpec(memory_space=pltpu.SMEM)
    hbm = pl.BlockSpec(memory_space=pl.ANY)
    f32 = jnp.float32
    out_tiles = jnp.swapaxes(out_tiles, 1, 2)
    arrays = (acts, out_grads, in_tiles, in_signs, out_tiles, out_signs, query_grads)
    tile = in_tiles.shape[1]
    shapes = [a.shape for a in arrays]
    shapes[0] = (in_tiles.shape[0],) + acts.shape[:2] + (tile,)
    shapes[1] = (out_tiles.shape[0],) + acts.shape[:2] + (tile,)
    slots = ex_count * inner
    return pl.pallas_call(
        functools.partial(body, seq_count, ex_count, inner),
        out_shape=jax.ShapeDtypeStruct((examples, queries), f32),
        in_specs=[smem] * 3 + [hbm] * 7,
        out_specs=pl.BlockSpec(memory_space=pltpu.VMEM),
        scratch_shapes=[pltpu.VMEM(shape, a.dtype) for shape, a in zip(shapes, arrays)]
        + [
            pltpu.VMEM((slots, piece_rows, lanes), f32),
            pltpu.VMEM((slots, piece_rows, lanes), f32),
            pltpu.VMEM((ex_count, piece_rows, lanes), f32),
            pltpu.VMEM((outer, ex_count, piece_rows, lanes), f32),
            pltpu.VMEM((gathered, lanes), f32),
            pltpu.VMEM((gathered, lanes), jnp.bfloat16),
            pltpu.VMEM((inner, gathered, lanes), jnp.bfloat16),
            pltpu.VMEM((ex_count, examples, queries), f32),
            pltpu.VMEM((ex_count, examples, queries), f32),
            pltpu.SemaphoreType.DMA((len(arrays),)),
            pltpu.SemaphoreType.DMA((slots,)),
            pltpu.SemaphoreType.DMA((slots,)),
            pltpu.SemaphoreType.DMA((outer,)),
            pltpu.SemaphoreType.DMA((outer,)),
            pltpu.SemaphoreType.DMA((inner,)),
            pltpu.SemaphoreType.DMA((inner,)),
            pltpu.SemaphoreType.DMA((ex_count,)),
            pltpu.SemaphoreType.DMA((ex_count,)),
        ],
        compiler_params=pltpu.CompilerParams(collective_id=0, has_side_effects=True),
        name="scores",
    )(lengths, in_blocks, out_blocks, *arrays)


def solution(mesh):
    in_specs = (
        P("ex", "seq", None),
        P("ex", "seq", None),
        P("ex"),
        P(),
        P(),
        P(),
        P(),
        P(),
        P(),
        P("seq", "ex"),
    )
    return jax.shard_map(
        functools.partial(per_device, mesh.shape["seq"], mesh.shape["ex"]),
        mesh=mesh,
        in_specs=in_specs,
        out_specs=P("ex", "seq"),
        check_vma=False,
    )
```

```python
import functools

import jax
import jax.numpy as jnp
from jax import lax
from jax.experimental import pallas as pl
from jax.experimental.pallas import tpu as pltpu
from jax.sharding import PartitionSpec as P

MESH = pl.DeviceIdType.MESH
SUBLANES = 16


def signed_columns(rows_ref, blocks_ref, signs_ref, first, count):
    signs = (2 * signs_ref[...] - 1).astype(jnp.float32).astype(jnp.bfloat16)
    columns = []
    for b in range(first, first + count):
        columns.append(rows_ref[blocks_ref[b]] * signs[b : b + 1, :])
    return jnp.concatenate(columns, axis=1)


def body(
    seq_count,
    ex_count,
    inner,
    lengths_ref,
    in_blocks_ref,
    out_blocks_ref,
    acts_hbm,
    grads_hbm,
    in_tiles_hbm,
    in_signs_hbm,
    out_tiles_hbm,
    out_signs_hbm,
    query_hbm,
    out_ref,
    acts,
    grads,
    in_tiles,
    in_signs,
    out_tiles,
    out_signs,
    query,
    pieces,
    a_recv,
    b_send,
    b_recv,
    ordered,
    c_send,
    c_recv,
    d_send,
    d_recv,
    load_sem,
    a_ssem,
    a_rsem,
    b_ssem,
    b_rsem,
    c_ssem,
    c_rsem,
    d_ssem,
    d_rsem,
):
    outer = seq_count // inner
    s = lax.axis_index("seq")
    x = lax.axis_index("ex")
    o = s // inner
    i = lax.rem(s, inner)

    loads = {}
    examples = len(acts)
    positions = acts[0].shape[1]
    for n, name, src, dst in (
        (0, "in_signs", in_signs_hbm, in_signs),
        (1, "out_signs", out_signs_hbm, out_signs),
        (2, "in_tiles", in_tiles_hbm, in_tiles),
        (5, "acts", acts_hbm, acts),
        (3, "out_tiles", out_tiles_hbm, out_tiles),
        (5 + examples, "grads", grads_hbm, grads),
    ):
        if not isinstance(dst, tuple):
            loads[name] = pltpu.make_async_copy(src, dst, load_sem.at[n])
            loads[name].start()
            continue
        for e, part in enumerate(dst):
            width = part.shape[2]
            for b in range(part.shape[0]):
                pltpu.make_async_copy(
                    src.at[e, :, b * width : (b + 1) * width], part.at[b], load_sem.at[n + e]
                ).start()
            loads[name, e] = pltpu.make_async_copy(part, part, load_sem.at[n + e])

    def at(outer_step, inner_step, ex_step):
        to_o = lax.rem(o + outer_step, outer)
        to_i = lax.rem(i + inner_step, inner)
        to_x = lax.rem(x + ex_step, ex_count)
        return to_o * inner + to_i, to_x

    near = [(di, dx) for dx in range(ex_count) for di in range(inner) if di or dx]
    barrier = pltpu.get_barrier_semaphore()
    peers = [(0, di, dx) for di, dx in near] + [(do, 0, 0) for do in range(1, outer)]
    for steps in peers:
        to_s, to_x = at(*steps)
        pl.semaphore_signal(barrier, 1, device_id=(to_s, to_x), device_id_type=MESH)

    in_count = in_tiles.shape[0]
    out_count = out_tiles.shape[0]
    cols = out_tiles.shape[1]
    f32 = jnp.float32

    loads["in_signs"].wait()
    loads["in_tiles"].wait()
    tiles = in_tiles[...].reshape(-1, in_tiles.shape[2])
    place = s * positions + lax.broadcasted_iota(jnp.int32, (positions, 1), 0)
    in_parts = []
    for e in range(examples):
        loads["acts", e].wait()
        left = signed_columns(acts[e], in_blocks_ref, in_signs, 0, in_count)
        in_sketched = jnp.dot(left, tiles, preferred_element_type=f32)
        in_parts.append(
            jnp.where(place < lengths_ref[e], in_sketched, 0.0).astype(jnp.bfloat16)
        )

    loads["out_signs"].wait()
    loads["out_tiles"].wait()
    spans = ((0, in_count), (in_count, out_count))
    half_tiles = [
        jnp.concatenate([out_tiles[b] for b in range(first, last)], axis=1)
        for first, last in spans
    ]

    half_rows = in_parts[0].shape[1] // 2
    piece_rows = pieces.shape[1]
    crossed = [[], []]
    for e in range(examples):
        loads["grads", e].wait()
        if e == examples - 1:
            loads["query"] = pltpu.make_async_copy(query_hbm, query, load_sem.at[4])
            loads["query"].start()
        out_part = jnp.concatenate(
            [
                lax.dot_general(
                    signed_columns(grads[e], out_blocks_ref, out_signs, first, last - first),
                    right,
                    (((1,), (1,)), ((), ())),
                    preferred_element_type=f32,
                ).astype(jnp.bfloat16)
                for right, (first, last) in zip(half_tiles, spans)
            ],
            axis=1,
        )
        full = lax.dot_general(
            in_parts[e], out_part, (((0,), (0,)), ((), ())), preferred_element_type=f32
        )
        full = full / lengths_ref[e].astype(f32)
        crossed[0].append(full[:half_rows, :cols])
        crossed[1].append(full[half_rows:, cols:])
    joined = jnp.concatenate([jnp.concatenate(part, axis=1) for part in crossed], axis=0)
    for p in range(pieces.shape[0]):
        pieces[p] = joined[p * piece_rows : (p + 1) * piece_rows]

    pl.semaphore_wait(barrier, len(peers))

    sends = []

    def push(src, dst, ssem, rsem, steps):
        to_s, to_x = at(*steps)
        copy = pltpu.make_async_remote_copy(
            src, dst, ssem, rsem, device_id=(to_s, to_x), device_id_type=MESH
        )
        copy.start()
        sends.append(copy)
        return copy

    got = {}
    for di, dx in near:
        to_i = lax.rem(i + di, inner)
        to_x = lax.rem(x + dx, ex_count)
        slot = dx * inner + di
        got[slot] = push(
            pieces.at[to_x * inner + to_i],
            a_recv.at[slot],
            a_ssem.at[slot],
            a_rsem.at[slot],
            (0, di, dx),
        )
    own = pieces[x * inner + i]
    for dx in range(ex_count):
        total = own if dx == 0 else None
        for di in range(inner):
            slot = dx * inner + di
            if slot == 0:
                continue
            got[slot].wait_recv()
            total = a_recv[slot] if total is None else total + a_recv[slot]
        b_send[dx] = total

    arrivals = [
        push(b_send, b_recv.at[do], b_ssem.at[do], b_rsem.at[do], (do, 0, 0))
        for do in range(1, outer)
    ]
    summed = b_send[...]
    for do, copy in enumerate(arrivals, 1):
        copy.wait_recv()
        summed = summed + b_recv[do]
    b_recv[0] = summed

    all_examples = ex_count * examples
    pairs = piece_rows // 2
    for dx in range(ex_count):
        even = b_recv[0, dx, pl.ds(0, pairs, stride=2), :]
        odd = b_recv[0, dx, pl.ds(1, pairs, stride=2), :]
        for e in range(examples):
            lanes = slice(e * cols, (e + 1) * cols)
            ordered[pl.ds(dx * examples + e, pairs, stride=all_examples), :] = jnp.concatenate(
                [even[:, lanes], odd[:, lanes]], axis=1
            )
    c_send[...] = ordered[...].astype(jnp.bfloat16)
    arrivals = [
        push(c_send, c_recv.at[di], c_ssem.at[di], c_rsem.at[di], (0, di, 0))
        for di in range(1, inner)
    ]

    loads["query"].wait()
    width = 2 * cols
    group = max(SUBLANES, all_examples)
    per_group = group // all_examples
    groups = c_send.shape[0] // group
    sums = [None] * per_group
    for di in range(inner):
        if di:
            arrivals[di - 1].wait_recv()
        from_i = lax.rem(i - di + inner, inner)
        chunk = c_recv[di] if di else c_send[...]
        left = jnp.concatenate(
            [chunk[u * group : (u + 1) * group] for u in range(groups)], axis=1
        )
        for j in range(per_group):
            right = jnp.concatenate(
                [
                    query[
                        :,
                        pl.ds(
                            pl.multiple_of((from_i * pairs + u * per_group + j) * width, width),
                            width,
                        ),
                    ]
                    for u in range(groups)
                ],
                axis=1,
            )
            term = lax.dot_general(
                left, right, (((1,), (1,)), ((), ())), preferred_element_type=f32
            )
            sums[j] = term if sums[j] is None else sums[j] + term
    scores = sums[0][:all_examples]
    for j in range(1, per_group):
        scores = scores + sums[j][j * all_examples : (j + 1) * all_examples]

    for dx in range(1, ex_count):
        d_send[dx] = scores[dx * examples : (dx + 1) * examples]
    arrivals = [
        push(
            d_send.at[dx], d_recv.at[dx], d_ssem.at[dx], d_rsem.at[dx], (0, 0, ex_count - dx)
        )
        for dx in range(1, ex_count)
    ]
    result = scores[:examples]
    for dx, copy in enumerate(arrivals, 1):
        copy.wait_recv()
        result = result + d_recv[dx]
    out_ref[...] = result
    for copy in sends:
        copy.wait_send()


def per_device(
    seq_count,
    ex_count,
    acts,
    out_grads,
    lengths,
    in_tiles,
    in_blocks,
    in_signs,
    out_tiles,
    out_blocks,
    out_signs,
    query_grads,
):
    examples = acts.shape[0]
    queries = query_grads.shape[0]
    in_cols = in_tiles.shape[2]
    cols = out_tiles.shape[2]
    inner = 4 if seq_count % 4 == 0 else 1
    outer = seq_count // inner
    piece_rows = in_cols // (ex_count * inner)
    lanes = examples * cols
    gathered = piece_rows // 2 * ex_count * examples
    smem = pl.BlockSpec(memory_space=pltpu.SMEM)
    hbm = pl.BlockSpec(memory_space=pl.ANY)
    f32 = jnp.float32
    out_tiles = jnp.swapaxes(out_tiles, 1, 2)
    arrays = (acts, out_grads, in_tiles, in_signs, out_tiles, out_signs, query_grads)
    tile = in_tiles.shape[1]
    held = [pltpu.VMEM(a.shape, a.dtype) for a in arrays]
    for n, tiles in ((0, in_tiles), (1, out_tiles)):
        part = pltpu.VMEM((tiles.shape[0], acts.shape[1], tile), arrays[n].dtype)
        held[n] = (part,) * examples
    slots = ex_count * inner
    return pl.pallas_call(
        functools.partial(body, seq_count, ex_count, inner),
        out_shape=pltpu.VMEM((examples, queries), f32),
        in_specs=[smem] * 3 + [hbm] * 7,
        out_specs=pl.BlockSpec(memory_space=pltpu.VMEM),
        scratch_shapes=held
        + [
            pltpu.VMEM((slots, piece_rows, lanes), f32),
            pltpu.VMEM((slots, piece_rows, lanes), f32),
            pltpu.VMEM((ex_count, piece_rows, lanes), f32),
            pltpu.VMEM((outer, ex_count, piece_rows, lanes), f32),
            pltpu.VMEM((gathered, lanes), f32),
            pltpu.VMEM((gathered, lanes), jnp.bfloat16),
            pltpu.VMEM((inner, gathered, lanes), jnp.bfloat16),
            pltpu.VMEM((ex_count, examples, queries), f32),
            pltpu.VMEM((ex_count, examples, queries), f32),
            pltpu.SemaphoreType.DMA((5 + 2 * examples,)),
            pltpu.SemaphoreType.DMA((slots,)),
            pltpu.SemaphoreType.DMA((slots,)),
            pltpu.SemaphoreType.DMA((outer,)),
            pltpu.SemaphoreType.DMA((outer,)),
            pltpu.SemaphoreType.DMA((inner,)),
            pltpu.SemaphoreType.DMA((inner,)),
            pltpu.SemaphoreType.DMA((ex_count,)),
            pltpu.SemaphoreType.DMA((ex_count,)),
        ],
        compiler_params=pltpu.CompilerParams(collective_id=0, has_side_effects=True),
        name="scores",
    )(lengths, in_blocks, out_blocks, *arrays)


def solution(mesh):
    in_specs = (
        P("ex", "seq", None),
        P("ex", "seq", None),
        P("ex"),
        P(),
        P(),
        P(),
        P(),
        P(),
        P(),
        P("seq", "ex"),
    )
    return jax.shard_map(
        functools.partial(per_device, mesh.shape["seq"], mesh.shape["ex"]),
        mesh=mesh,
        in_specs=in_specs,
        out_specs=P("ex", "seq"),
        check_vma=False,
    )
```
